256 devices in a mesh: req: 32 (over z_lo, x, y), tp: 8 (over z_hi, core).
Axes of the slice: x: 4, y: 4, z: 8 (z_hi: 4, z_lo: 2; z = z_hi * 2 + z_lo), core: 2. Of those that a mesh axis runs over, the one named last changes fastest.
Arguments:
- queries: bfloat16 [32768, 5120], P('req', 'tp')
- keys: bfloat16 [32768, 5120], P('req', 'tp')
- values: bfloat16 [32768, 5120], P('req', 'tp'), may hold values from -6 to 6
- cross_queries: bfloat16 [32768, 5120], P('req', 'tp')
- text_kv: bfloat16 [1024, 2, 5120], P(('req', 'tp'))
- segment_ids: int32 [32, 1024], P('req'), may hold values from 0 to 5, never falling along the last dimension, each value on 1 to 682 neighbouring positions
- prompt_of: int32 [32], P('req'), may hold values from 0 to 1
- page_owner: int32 [2048, 1], P('req'), may hold values from 0 to 31; in each aligned block of 64 rows (0 to 63, 64 to 127, ...) at most 3 rows name the same one
Outputs:
- self_out: bfloat16 [32768, 5120], P('req', 'tp')
- cross_out: bfloat16 [32768, 5120], P('req', 'tp')
- cache: bfloat16 [49152, 2, 5120], P('req', None, 'tp')
The draws below stay inside these ranges and needn't reach their ends.
Inputs may be any that keep to these rules, and one draw needn't show every extreme that they name: `page_owner`: among the pages of one stream (an aligned block of 64 rows), no device index appears more than 3 times; in some streams one appears exactly 3 times.
All inputs are finite; a program needn't handle non-finite values.
Results may differ from the reference program's by a relative error of at most 0.003.
The reference program's roundings to bfloat16 on the way count: a program that leaves them out, or rounds other values in their place, can miss the bound.
Values may be sent and summed in bfloat16 or wider, within the bound.
A program may use at most 128 MiB of HBM per device.

```python
import math
import jax
import jax.numpy as jnp
import numpy as np
from jax import lax

HEADS = 40
HEAD = 128
TEXT = 512
STREAM = 1024
SEGS = 6
PAGE = 16
PROMPTS = 2
SEG_MOST = 682
TOKENS = 32768
CAP = 3
N_REQ = 32


def column_scale(key, width, ceiling):
    place = jnp.arange(width).astype(jnp.float32) / (width - 1)
    jitter = jnp.exp(jax.random.uniform(key, (width,), jnp.float32, -0.35, 0.35))
    return jnp.exp(place * math.log(ceiling)) * jitter


def row_scale(key, count, ceiling):
    return jnp.exp(jax.random.uniform(key, (count, 1), jnp.float32, 0.0, math.log(ceiling)))


def rough_field(key, count, width):
    splits = jax.random.split(key, 3)
    base = jax.random.normal(splits[0], (count, width), jnp.float32)
    return base * column_scale(splits[1], width, 10.0) * row_scale(splits[2], count, 10.0)


def self_pair(key):
    width = HEADS * HEAD
    splits = jax.random.split(jax.random.fold_in(key, 101), 2)
    query_field = rough_field(splits[0], TOKENS, width)
    key_field = rough_field(splits[1], TOKENS, width)
    return (query_field, key_field)


def draw_queries(key, part):
    return self_pair(key)[0].astype(jnp.bfloat16)


def draw_keys(key, part):
    return self_pair(key)[1].astype(jnp.bfloat16)


def draw_cross_queries(key, part):
    width = HEADS * HEAD
    splits = jax.random.split(jax.random.fold_in(key, 303), 1)
    field = rough_field(splits[0], TOKENS, width)
    return field.astype(jnp.bfloat16)


def draw_text_kv(key, part):
    width = HEADS * HEAD
    count = PROMPTS * TEXT
    splits = jax.random.split(jax.random.fold_in(key, 404), 2)
    text_keys = rough_field(splits[0], count, width)
    text_values = 2.0 * jax.random.normal(splits[1], (count, width), jnp.float32)
    return jnp.stack([text_keys, text_values], axis=1).astype(jnp.bfloat16)


def set_ends(result, rng, least, high):
    spot = [jax.random.randint(jax.random.fold_in(rng, axis), (), 0, length) for axis, length in enumerate(result.shape)]
    widest = result.shape.index(max(result.shape))
    beside = spot[:widest] + [(spot[widest] + 1) % result.shape[widest]] + spot[widest + 1:]
    return result.at[tuple(spot)].set(least).at[tuple(beside)].set(high)


def block_scale(own_key, shape, cuts, smallest, largest):
    factor_of = 1.0
    for axis_at, blocks in cuts:
        steps = jax.random.uniform(jax.random.fold_in(jax.random.fold_in(own_key, 6), axis_at), (blocks,), jnp.float32, smallest / len(cuts), largest / len(cuts))
        factor_of = factor_of * jnp.repeat(jnp.exp(steps), shape[axis_at] // blocks).reshape((-1,) + (1,) * (len(shape) - 1 - axis_at))
    return factor_of


def split_up(count, total, limit, skew):
    portions = [(1 << 20) // math.isqrt(rank ** skew) + 1 for rank in range(2, count + 1)]
    surplus, counts = total - limit - (count - 1), [1] * (count - 1)
    while surplus > 0:
        candidates = [i for i in range(count - 1) if counts[i] < limit]
        mass, budget = sum([portions[i] for i in candidates]), surplus
        for i in candidates:
            more = min(limit - counts[i], max(1, budget * portions[i] // mass), surplus)
            counts[i] = counts[i] + more
            surplus = surplus - more
    return np.array([limit] + counts)


def ragged_sizes(key, amount, total, most, lean):
    if amount == 2:
        one = jax.random.randint(key, (), max(1, total - most), min(most, total - 1) + 1)
        return jnp.stack([one, total - one])
    lengths = jnp.asarray(split_up(amount, total, most, lean), jnp.int32)
    couples = (amount - 1) // 2
    donor, taker = lengths[1:1 + 2 * couples:2], lengths[2:2 + 2 * couples:2]
    room = jnp.minimum(donor - 1, most - taker)
    moved = jax.random.randint(jax.random.fold_in(key, 1), (couples,), 0, 1 << 20) % (room + 1)
    lengths = lengths.at[1:1 + 2 * couples:2].set(donor - moved).at[2:2 + 2 * couples:2].set(taker + moved)
    return lengths[jax.random.permutation(jax.random.fold_in(key, 2), amount)]


def assign_block(own_key, own, number, rows, number_of, top, limit, lean):
    order = jax.random.permutation(own_key, number_of)
    heavy_load, usual = load_shares(number_of, rows * top, limit, lean, True), load_shares(number_of, rows * top, limit, lean, False)
    places = jnp.arange(number_of)

    def named(lengths, offset_by):
        used = int((lengths > 0).sum())
        fixed = max(1, used // 4)
        moved = fixed + (places - fixed + offset_by * (used - fixed)) % max(1, number_of - fixed)
        return jnp.zeros((number_of,), jnp.int32).at[order[jnp.where(places < fixed, places, moved)]].set(jnp.asarray(lengths, jnp.int32))

    lengths = jnp.where(number % 4 == 0, named(heavy_load, number // 4), named(usual, number - number // 4 - 1))
    mixed = jax.random.permutation(jax.random.fold_in(own, 3), number_of)
    giver, sink = mixed[0:number_of // 2 * 2:2], mixed[1:number_of // 2 * 2:2]
    slack = jnp.minimum(lengths[giver] - 1, limit - lengths[sink]) // 2
    slack = jnp.where((giver == order[0]) | (sink == order[0]) | (lengths[sink] == 0), 0, jnp.maximum(slack, 0))
    moved = jax.random.randint(jax.random.fold_in(own, 4), (number_of // 2,), 0, 1 << 20) % (slack + 1)
    lengths = lengths.at[giver].add(-moved).at[sink].add(moved)
    members = jnp.searchsorted(jnp.cumsum(lengths), jnp.arange(rows * top), side="right").astype(jnp.int32)
    grid = members.reshape(top, rows).T
    grid = grid[jax.random.permutation(jax.random.fold_in(own, 1), rows)]
    offset_by = jax.random.randint(jax.random.fold_in(own, 2), (rows, 1), 0, top)
    return jnp.take_along_axis(grid, (jnp.arange(top)[None, :] + offset_by) % top, axis=1)


def load_shares(count, total, most, lean, full):
    portions = [(1 << 20) // math.isqrt(grade ** lean) + 1 for grade in range(1, count + 1)]
    largest = most if full else min(most, max(-(-total // count), total * portions[0] // sum(portions)))
    least = 1 if total - largest >= count - 1 else 0
    counts, spare = [largest] + [least] * (count - 1), total - largest - least * (count - 1)
    while spare > 0:
        movable = [i for i in range(1, count) if counts[i] < largest] or [i for i in range(1, count) if counts[i] < most]
        whole, left = sum([portions[i] for i in movable]), spare
        for i in movable:
            more = min(most - counts[i], max(1, left * portions[i] // whole), spare)
            counts[i] = counts[i] + more
            spare = spare - more
    return np.array(counts)


def bell_draw(stream_key, shape, scale, reach, pieces=(), held_as=jnp.bfloat16):
    result = scale * jax.random.normal(stream_key, shape, jnp.float32)
    if pieces:
        result = result * block_scale(stream_key, shape, pieces, -0.22, 0.18)
    return jnp.clip(result, -reach, reach).astype(held_as)


def setup_inputs(seed: int = 0) -> dict:
    key_of = jax.random.split(jax.random.key(seed), 9)
    queries = draw_queries(jax.random.fold_in(key_of[8], 71), 0)
    keys = draw_keys(jax.random.fold_in(key_of[8], 71), 0)
    values = bell_draw(key_of[2], (TOKENS, HEADS * HEAD), 2.0, 6.0, ((0, 32), (1, 8)))
    cross_queries = draw_cross_queries(jax.random.fold_in(key_of[8], 71), 0)
    text_kv = draw_text_kv(jax.random.fold_in(key_of[8], 71), 0)
    segment_ids = jax.vmap(lambda own: jnp.searchsorted(jnp.cumsum(ragged_sizes(own, SEGS, STREAM, SEG_MOST, 2)), jnp.arange(STREAM), side="right"))(jax.random.split(key_of[5], N_REQ)).reshape((N_REQ, STREAM)).astype(jnp.int32)
    prompt_of = set_ends(jax.random.randint(key_of[6], (N_REQ,), 0, PROMPTS), jax.random.fold_in(key_of[6], 1), 0, PROMPTS - 1).astype(jnp.int32)
    page_owner_keys = jax.random.split(jax.random.fold_in(key_of[7], 1), (N_REQ * (STREAM // PAGE)) // (STREAM // PAGE))
    page_owner_turns = jax.random.permutation(jax.random.fold_in(key_of[7], 3), (N_REQ * (STREAM // PAGE)) // (STREAM // PAGE))
    page_owner = jax.vmap(lambda own, number: assign_block(jax.random.fold_in(key_of[7], 2), own, number, STREAM // PAGE, N_REQ, 1, CAP, 1))(page_owner_keys, page_owner_turns).reshape((N_REQ * (STREAM // PAGE), 1))
    return dict(queries=queries, keys=keys, values=values, cross_queries=cross_queries, text_kv=text_kv, segment_ids=segment_ids, prompt_of=prompt_of, page_owner=page_owner)


EPSILON = 1e-06
NEGATIVE = -1e+30

def normalized(block):
    wide = block.astype(jnp.float32)
    factor = lax.rsqrt(lax.optimization_barrier(jnp.sum(wide * wide, axis=-1, keepdims=True)) / (HEADS * HEAD) + EPSILON)
    return (wide * factor).astype(jnp.bfloat16)

def head_softmax(query_rows, key_rows, value_rows, allowed):
    scores = jnp.dot(query_rows, key_rows.T, preferred_element_type=jnp.float32) * HEAD ** (-0.5)
    masked = jnp.where(allowed, scores, NEGATIVE)
    row_top = lax.optimization_barrier(jnp.max(masked, axis=1, keepdims=True))
    weights = jnp.where(allowed, jnp.exp(masked - row_top), 0.0)
    row_total = lax.optimization_barrier(jnp.sum(weights, axis=1, keepdims=True))
    summed = jnp.dot(weights.astype(jnp.bfloat16), value_rows, preferred_element_type=jnp.float32)
    return summed / row_total

def split_heads(rows):
    return rows.reshape(rows.shape[0], HEADS, HEAD).transpose(1, 0, 2)

def join_heads(stacked):
    return stacked.transpose(1, 0, 2).reshape(stacked.shape[1], HEADS * HEAD).astype(jnp.bfloat16)

def reference(queries, keys, values, cross_queries, text_kv, segment_ids, prompt_of, page_owner):
    query_hat = normalized(queries)
    key_hat = normalized(keys)
    cross_hat = normalized(cross_queries)
    text_hat = normalized(text_kv[:, 0, :])
    text_values = text_kv[:, 1, :]

    def one_stream(stream_index):
        offset = (stream_index * STREAM).astype(jnp.int32)
        query_rows = lax.dynamic_slice_in_dim(query_hat, offset, STREAM, 0)
        key_rows = lax.dynamic_slice_in_dim(key_hat, offset, STREAM, 0)
        value_rows = lax.dynamic_slice_in_dim(values, offset, STREAM, 0)
        cross_rows = lax.dynamic_slice_in_dim(cross_hat, offset, STREAM, 0)
        segments = segment_ids[stream_index]
        allowed = segments[:, None] == segments[None, :]
        self_heads = lax.map(lambda parts: head_softmax(parts[0], parts[1], parts[2], allowed), (split_heads(query_rows), split_heads(key_rows), split_heads(value_rows)))
        start = (prompt_of[stream_index] * TEXT).astype(jnp.int32)
        prompt_keys = lax.dynamic_slice_in_dim(text_hat, start, TEXT, 0)
        prompt_values = lax.dynamic_slice_in_dim(text_values, start, TEXT, 0)
        everywhere = jnp.ones((1, TEXT), dtype=jnp.bool_)
        cross_heads = lax.map(lambda parts: head_softmax(parts[0], parts[1], parts[2], everywhere), (split_heads(cross_rows), split_heads(prompt_keys), split_heads(prompt_values)))
        return (join_heads(self_heads), join_heads(cross_heads))
    self_all, cross_all = lax.map(one_stream, jnp.arange(N_REQ, dtype=jnp.int32))
    self_out = self_all.reshape(TOKENS, HEADS * HEAD)
    cross_out = cross_all.reshape(TOKENS, HEADS * HEAD)
    pages = STREAM // PAGE
    owners = page_owner[:, 0].reshape(N_REQ, pages).astype(jnp.int32)
    same_owner = owners[:, :, None] == owners[:, None, :]
    before = lax.broadcasted_iota(jnp.int32, (pages, pages), 1) < lax.broadcasted_iota(jnp.int32, (pages, pages), 0)
    rank = lax.optimization_barrier(jnp.sum(jnp.where(jnp.logical_and(same_owner, before[None]), 1, 0), axis=2)).astype(jnp.int32)
    stream_ids = jnp.arange(N_REQ, dtype=jnp.int32)[:, None]
    page_rows = owners * (N_REQ * CAP * PAGE) + stream_ids * (CAP * PAGE) + rank * PAGE
    target = (page_rows[:, :, None] + jnp.arange(PAGE, dtype=jnp.int32)[None, None, :]).reshape(TOKENS)
    stacked = jnp.stack([key_hat, values], axis=1)
    cache = jnp.zeros((N_REQ * N_REQ * CAP * PAGE, 2, HEADS * HEAD), jnp.bfloat16).at[target].set(stacked)
    return (self_out, cross_out, cache)
```

```python
import functools
import math

import jax
import jax.numpy as jnp
import numpy as np
from jax import lax
from jax.experimental import pallas as pl
from jax.experimental.layout import Layout, with_layout_constraint
from jax.experimental.pallas import tpu as pltpu
from jax.sharding import PartitionSpec as P

HEADS = 40
HEAD = 128
TEXT = 512
PAGE = 16
CAP = 3
NREQ = 32
NTP = 8
STREAM = 1024
PAGES = STREAM // PAGE
LOCAL = HEADS // NTP
WIDTH = HEADS * HEAD
EPSILON = 1e-06
NEGATIVE = -1e30
MESH = pl.DeviceIdType.MESH
TOK = 4
PART = 48
QBLOCK = 256


def page_order():
    rows = 2 * LOCAL * PAGE
    place = np.zeros((rows, rows), np.float32)
    for token in range(PAGE):
        for head in range(LOCAL):
            for kv in range(2):
                place[(token * LOCAL + head) * 2 + kv, (head * 2 + kv) * PAGE + token] = 1
    return place


def split_order():
    place = np.zeros((NTP * PART, TOK * HEADS * 2), np.float32)
    for part in range(NTP):
        for kv in range(2):
            for head in range(LOCAL):
                for token in range(TOK):
                    row = part * PART + (kv * LOCAL + head) * TOK + token
                    place[row, (token * HEADS + part * LOCAL + head) * 2 + kv] = 1
    return place


def join_order():
    place = np.zeros((2 * LOCAL * NTP * TOK, NTP * PART), np.float32)
    for part in range(NTP):
        for lead in range(2 * LOCAL):
            for token in range(TOK):
                place[lead * NTP * TOK + part * TOK + token, part * PART + lead * TOK + token] = 1
    return place


def kernel(
    source_ref, prompt_ref, q_hbm, k_hbm, v_hbm, c_hbm, text_hbm, seg_ref, page_ref, split_ref, join_ref,
    cache_ref, self_ref, cross_ref,
    q5, k5, v5, c5, text, sums, factor, part_out, part_in, text_k, text_v, outgoing, segcol, bias,
    load_sem, store_sem, sum_send, sum_recv, part_send, part_recv,
    k1_send, k1_recv, v1_send, v1_recv, k2_send, k2_recv, v2_send, v2_recv, page_send, page_recv,
):
    req = lax.axis_index("req")
    tp = lax.axis_index("tp")
    z, x, y = req // 16, (req // 4) % 4, req % 4

    def at(dz, dx, dy):
        return ((z + dz) % 2) * 16 + ((x + dx) % 4) * 4 + (y + dy) % 4

    def remote(src, dst, send, recv, req_to, tp_to):
        return pltpu.make_async_remote_copy(
            src_ref=src, dst_ref=dst, send_sem=send, recv_sem=recv,
            device_id=(req_to, tp_to), device_id_type=MESH,
        )

    def load(index, src, dst):
        copy = pltpu.make_async_copy(src, dst, load_sem.at[index])
        copy.start()
        return copy

    text_load = load(0, text_hbm, text)
    loads = []
    for which, (hbm, buf) in enumerate(((k_hbm, k5), (q_hbm, q5), (c_hbm, c5), (v_hbm, v5))):
        for h in range(LOCAL):
            loads.append(
                load(1 + which * LOCAL + h, hbm.at[:, :, pl.ds(h * HEAD, HEAD)], buf.at[h, pl.ds(0, PAGES)])
            )

    barrier = pltpu.get_barrier_semaphore()

    @pl.loop(1, NREQ)
    def _(d):
        pl.semaphore_signal(barrier, inc=1, device_id=((req + d) % NREQ, tp), device_id_type=MESH)

    @pl.loop(1, NTP)
    def _(d):
        pl.semaphore_signal(barrier, inc=1, device_id=(req, (tp + d) % NTP), device_id_type=MESH)

    for h in range(LOCAL):
        k5[h, PAGES] = jnp.zeros((PAGE, HEAD), jnp.bfloat16)
        v5[h, PAGES] = jnp.zeros((PAGE, HEAD), jnp.bfloat16)

    text_load.wait()
    per = HEADS * 2
    even = lax.broadcasted_iota(jnp.int32, (per, HEAD), 0) % 2 == 0
    normed = []
    for token in range(TOK):
        rows = text[token * per : (token + 1) * per, :].astype(jnp.float32)
        keyed = jnp.where(even, rows, 0.0)
        total = jnp.sum(jnp.sum(keyed * keyed, axis=0, keepdims=True), axis=1, keepdims=True)
        scaled = rows * lax.rsqrt(total / WIDTH + EPSILON)
        normed.append(jnp.where(even, scaled, rows).astype(jnp.bfloat16))
    parts = jnp.dot(split_ref[...], jnp.concatenate(normed, axis=0), preferred_element_type=jnp.float32)
    part_out[...] = parts.astype(jnp.bfloat16).reshape(NTP, PART, HEAD)
    part_in[tp] = part_out[tp]

    pl.semaphore_wait(barrier, NREQ - 1 + NTP - 1)

    def part_copy(d):
        other = (tp + d) % NTP
        return remote(part_out.at[other], part_in.at[tp], part_send.at[d], part_recv.at[d], req, other)

    @pl.loop(1, NTP)
    def _(d):
        part_copy(d).start()

    for which, buf in enumerate((k5, q5, c5)):
        for h in range(LOCAL):
            loads[which * LOCAL + h].wait()

        @pl.loop(0, 8)
        def _(b, which=which, buf=buf):
            acc = jnp.zeros((128, HEAD), jnp.float32)
            for h in range(LOCAL):
                wide = buf[h, pl.ds(b * 8, 8)].reshape(128, HEAD).astype(jnp.float32)
                acc = acc + wide * wide
            sums[tp, which, pl.ds(b, 1), :] = jnp.sum(acc.T, axis=0, keepdims=True)

    def sum_copy(d):
        other = (tp + d) % NTP
        return remote(sums.at[tp], sums.at[tp], sum_send.at[d], sum_recv.at[d], req, other)

    @pl.loop(1, NTP)
    def _(d):
        sum_copy(d).start()

    @pl.loop(1, NTP)
    def _(d):
        part_copy(d).wait()

    block = jnp.dot(join_ref[...], part_in[...].reshape(NTP * PART, HEAD), preferred_element_type=jnp.float32)
    block = block.astype(jnp.bfloat16)
    half = LOCAL * NTP * TOK
    text_k[z, x, y] = block[:half]
    text_v[z, x, y] = block[half:]

    def k1_copy(d):
        own = text_k.at[z, x, y]
        return remote(own, own, k1_send.at[d], k1_recv.at[d], at(d // 4, d % 4, 0), tp)

    def v1_copy(d):
        own = text_v.at[z, x, y]
        return remote(own, own, v1_send.at[d], v1_recv.at[d], at(d // 4, 0, d % 4), tp)

    def k2_copy(d, e):
        held = text_k.at[(z - d // 4 + 2) % 2, (x - d % 4 + 4) % 4, y]
        spot = d * 3 + e - 1
        return remote(held, held, k2_send.at[spot], k2_recv.at[spot], at(0, 0, e), tp)

    def v2_copy(d, e):
        held = text_v.at[(z - d // 4 + 2) % 2, x, (y - d % 4 + 4) % 4]
        spot = d * 3 + e - 1
        return remote(held, held, v2_send.at[spot], v2_recv.at[spot], at(0, e, 0), tp)

    @pl.loop(1, 8)
    def _(d):
        k1_copy(d).start()
        v1_copy(d).start()

    @pl.loop(1, NTP)
    def _(d):
        sum_copy(d).wait()

    total = sums[0]
    for t in range(1, NTP):
        total = total + sums[t]
    factor[...] = lax.rsqrt(total / WIDTH + EPSILON)

    def normalize(which, buf):
        @pl.loop(0, 8)
        def _(b):
            column = jnp.broadcast_to(factor[which, pl.ds(b, 1), :], (128, HEAD)).T
            for h in range(LOCAL):
                wide = buf[h, pl.ds(b * 8, 8)].reshape(128, HEAD).astype(jnp.float32)
                buf[h, pl.ds(b * 8, 8)] = (wide * column).astype(jnp.bfloat16).reshape(8, PAGE, HEAD)

    normalize(0, k5)
    for h in range(LOCAL):
        loads[3 * LOCAL + h].wait()

    @pl.loop(0, 8)
    def _(d):
        @pl.when(d > 0)
        def _():
            k1_copy(d).wait()
            v1_copy(d).wait()

        for e in range(1, 4):
            k2_copy(d, e).start()
            v2_copy(d, e).start()

    def dest(i):
        d = (i * 11) % NREQ
        return at(d // 16, (d // 4) % 4, d % 4), d

    def build(i):
        to, _ = dest(i)
        for j in range(CAP):
            slot = to * CAP + j
            page = source_ref[slot]
            rows = jnp.concatenate([buf[h, page] for h in range(LOCAL) for buf in (k5, v5)], axis=0)
            placed = jnp.dot(page_ref[...], rows, preferred_element_type=jnp.float32)
            outgoing[slot] = placed.astype(jnp.bfloat16)

    def page_copy(i, j):
        to, d = dest(i)
        return remote(
            outgoing.at[to * CAP + j], cache_ref.at[req * CAP + j],
            page_send.at[d * CAP + j], page_recv.at[d * CAP + j], to, tp,
        )

    build(0)
    own = pltpu.make_async_copy(
        outgoing.at[pl.ds(req * CAP, CAP)], cache_ref.at[pl.ds(req * CAP, CAP)], store_sem.at[2 * LOCAL]
    )
    build(1)
    own.start()

    @pl.loop(1, NREQ - 1)
    def _(i):
        build(i + 1)
        for j in range(CAP):
            page_copy(i, j).start()

    normalize(1, q5)
    for j in range(CAP):
        page_copy(NREQ - 1, j).start()
    normalize(2, c5)

    power = HEAD ** (-0.5) * math.log2(math.e)
    qpages = QBLOCK // PAGE

    def soften(scores, values):
        top = jnp.max(scores, axis=1, keepdims=True)
        weights = jnp.exp2(scores - top)
        total = jnp.sum(weights, axis=1, keepdims=True)
        product = jnp.dot(weights.astype(jnp.bfloat16), values, preferred_element_type=jnp.float32)
        return (product / total).astype(jnp.bfloat16)

    for b in range(8):
        lane = seg_ref[:, b * 128 : (b + 1) * 128].astype(jnp.float32)
        segcol[b * 128 : (b + 1) * 128, :] = jnp.broadcast_to(lane, (128, 128)).T

    contract = (((1,), (1,)), ((), ()))

    @pl.loop(0, STREAM // QBLOCK)
    def _(b):
        mine = segcol[pl.ds(b * QBLOCK, QBLOCK), :]
        for j in range(STREAM // 128):
            lane = seg_ref[:, j * 128 : (j + 1) * 128].astype(jnp.float32)
            bias[:, j * 128 : (j + 1) * 128] = jnp.where(mine == lane, 0.0, NEGATIVE)

        @pl.loop(0, LOCAL)
        def _(h):
            rows = q5[h, pl.ds(b * qpages, qpages)].reshape(QBLOCK, HEAD)
            keys = k5[h, pl.ds(0, PAGES)].reshape(STREAM, HEAD)
            scores = lax.dot_general(rows, keys, contract, preferred_element_type=jnp.float32)
            done = soften(scores * power + bias[...], v5[h, pl.ds(0, PAGES)].reshape(STREAM, HEAD))
            q5[h, pl.ds(b * qpages, qpages)] = done.reshape(qpages, PAGE, HEAD)

    stores = []
    for h in range(LOCAL):
        copy = pltpu.make_async_copy(q5.at[h], self_ref.at[:, :, pl.ds(h * HEAD, HEAD)], store_sem.at[h])
        copy.start()
        stores.append(copy)

    @pl.loop(0, 8)
    def _(d):
        for e in range(1, 4):
            k2_copy(d, e).wait()
            v2_copy(d, e).wait()

    prompt = prompt_ref[0]

    @pl.loop(0, STREAM // QBLOCK)
    def _(b):
        @pl.loop(0, LOCAL)
        def _(h):
            tokens = NTP * TOK
            keys = text_k[prompt, :, :, pl.ds(h * tokens, tokens)].reshape(TEXT, HEAD)
            values = text_v[prompt, :, :, pl.ds(h * tokens, tokens)].reshape(TEXT, HEAD)
            rows = c5[h, pl.ds(b * qpages, qpages)].reshape(QBLOCK, HEAD)
            scores = lax.dot_general(rows, keys, contract, preferred_element_type=jnp.float32)
            done = soften(scores * power, values)
            c5[h, pl.ds(b * qpages, qpages)] = done.reshape(qpages, PAGE, HEAD)

    for h in range(LOCAL):
        copy = pltpu.make_async_copy(c5.at[h], cross_ref.at[:, :, pl.ds(h * HEAD, HEAD)], store_sem.at[LOCAL + h])
        copy.start()
        stores.append(copy)

    @pl.loop(1, NREQ)
    def _(i):
        for j in range(CAP):
            page_copy(i, j).wait()

    own.wait()
    for copy in stores:
        copy.wait()


def per_device(queries, keys, values, cross_queries, text_kv, segment_ids, prompt_of, page_owner):
    owners = page_owner[:, 0]
    before = lax.broadcasted_iota(jnp.int32, (PAGES, PAGES), 1) < lax.broadcasted_iota(
        jnp.int32, (PAGES, PAGES), 0
    )
    same = owners[:, None] == owners[None, :]
    rank = jnp.sum(jnp.where(jnp.logical_and(same, before), 1, 0), axis=1).astype(jnp.int32)
    slot = owners * CAP + rank
    hit = lax.broadcasted_iota(jnp.int32, (NREQ * CAP, PAGES), 0) == slot[None, :]
    number = lax.broadcasted_iota(jnp.int32, (NREQ * CAP, PAGES), 1)
    source = PAGES + jnp.sum(jnp.where(hit, number - PAGES, 0), axis=1).astype(jnp.int32)

    paged = lambda a: a.reshape(PAGES, PAGE, LOCAL * HEAD)
    text = text_kv.reshape(TOK, 2, HEADS, HEAD).transpose(0, 2, 1, 3).reshape(TOK * HEADS * 2, HEAD)
    consts = [jnp.asarray(make(), jnp.bfloat16) for make in (page_order, split_order, join_order)]
    rows = PAGE * LOCAL * 2
    out = jax.ShapeDtypeStruct((PAGES, PAGE, LOCAL * HEAD), jnp.bfloat16)
    hbm = pl.BlockSpec(memory_space=pltpu.HBM)
    vmem = pl.BlockSpec(memory_space=pltpu.VMEM)
    smem = pl.BlockSpec(memory_space=pltpu.SMEM)
    dma = lambda count: pltpu.SemaphoreType.DMA((count,))
    heads = lambda pages: pltpu.VMEM((LOCAL, pages, PAGE, HEAD), jnp.bfloat16)
    block = pltpu.VMEM((2, 4, 4, LOCAL * NTP * TOK, HEAD), jnp.bfloat16)
    cache, self_out, cross_out = pl.pallas_call(
        kernel,
        out_shape=(jax.ShapeDtypeStruct((NREQ * CAP, rows, HEAD), jnp.bfloat16), out, out),
        in_specs=[smem, smem, hbm, hbm, hbm, hbm, hbm, vmem, vmem, vmem, vmem],
        out_specs=(hbm, hbm, hbm),
        scratch_shapes=[
            heads(PAGES), heads(PAGES + 1), heads(PAGES + 1), heads(PAGES),
            pltpu.VMEM((TOK * HEADS * 2, HEAD), jnp.bfloat16),
            pltpu.VMEM((NTP, 3, 8, 128), jnp.float32),
            pltpu.VMEM((3, 8, 128), jnp.float32),
            pltpu.VMEM((NTP, PART, HEAD), jnp.bfloat16),
            pltpu.VMEM((NTP, PART, HEAD), jnp.bfloat16),
            block, block,
            pltpu.VMEM((NREQ * CAP, rows, HEAD), jnp.bfloat16),
            pltpu.VMEM((STREAM, 128), jnp.float32),
            pltpu.VMEM((QBLOCK, STREAM), jnp.float32),
            dma(1 + 4 * LOCAL), dma(2 * LOCAL + 1), dma(NTP), dma(NTP), dma(NTP), dma(NTP),
            dma(8), dma(8), dma(8), dma(8), dma(24), dma(24), dma(24), dma(24),
            dma(NREQ * CAP), dma(NREQ * CAP),
        ],
        compiler_params=pltpu.CompilerParams(
            collective_id=0, has_side_effects=True, vmem_limit_bytes=56 * 2**20
        ),
    )(
        source, prompt_of, paged(queries), paged(keys), paged(values), paged(cross_queries), text,
        segment_ids, *consts,
    )
    cache = cache.reshape(NREQ * CAP * PAGE, LOCAL, 2, HEAD).transpose(0, 2, 1, 3)
    cache = with_layout_constraint(cache, Layout(major_to_minor=(0, 2, 1, 3)))
    flat = lambda a: a.reshape(STREAM, LOCAL * HEAD)
    return flat(self_out), flat(cross_out), cache.reshape(NREQ * CAP * PAGE, 2, LOCAL * HEAD)


def solution(mesh):
    placed = (
        P("req", "tp"),
        P("req", "tp"),
        P("req", "tp"),
        P("req", "tp"),
        P(("req", "tp"), None, None),
        P("req", None),
        P("req"),
        P("req", None),
    )
    return jax.shard_map(
        per_device,
        mesh=mesh,
        in_specs=placed,
        out_specs=(P("req", "tp"), P("req", "tp"), P("req", None, "tp")),
        check_vma=False,
    )
```
